32 devices in a mesh: ctx: 16 (over z, y, core), doc: 2 (over x).
Axes of the slice: x: 2, y: 2, z: 4, core: 2. Of those that a mesh axis runs over, the one named last changes fastest.
Arguments:
- activations: float32 [2, 4096, 1024], P('doc', 'ctx'), may hold values from -60 to 60
- queries: float32 [2, 4096, 512], P('doc', 'ctx'), may hold values from -8 to 8
- d_out: float32 [2, 4096, 512], P('doc', 'ctx'), may hold values from -6 to 6
- w_kv: float32 [1024, 1024], replicated, may hold values from -1 to 1
- partner: int32 [2, 16], P('doc', 'ctx'), may hold values from 0 to 15, as said below
- block_mask: int32 [2, 16, 4, 4], P('doc', 'ctx'), may hold values from 0 to 1, as said below
Outputs:
- attended: float32 [2, 4096, 512], P('doc', 'ctx')
- grad_w_kv: float32 [1024, 1024], P('ctx', 'doc')
The draws below stay inside these ranges and needn't reach their ends.
Inputs may be any that keep to these rules, and one draw needn't show every extreme that they name: partner[d, i] = i XOR s_d, where s_d of 1 to 15 is the same for all shards of document d, so shards are matched in pairs. `block_mask`: any 0/1 values; a shard's mask may be all zero or all one, and partners' masks are independent.
All inputs are finite; a program needn't handle non-finite values.
Results may differ from the reference program's by a relative error of at most 0.0003.
Values sent between devices are 32-bit elements; how exact they have to be, the bound alone decides.
No kernel may reach another device: no remote copies, remote signals or barrier semaphores. Data moves between devices by JAX's collectives and lax.ppermute only.
A program may use at most 64 MiB of HBM per device.

```python
import math
import jax
import jax.numpy as jnp
from jax import lax

D = 1024
HEAD = 64
TOK_DEV = 256
KW = 512
NB = 4
SEQ = 4096
DOCS = 2
TOKENS = 8192
N_CTX = 16


def draw_w_kv(key, part):
    values = jax.random.normal(jax.random.fold_in(key, 22), (D, 2 * KW), jnp.float32)
    return jnp.clip(values, -3.0, 3.0) / math.sqrt(D)


def draw_activations(key, part):
    values = jnp.clip(jax.random.normal(jax.random.fold_in(key, 23), (DOCS, SEQ, D), jnp.float32), -4.0, 4.0)
    return jnp.clip(values, -60.0, 60.0)


def draw_queries(key, part):
    values = jnp.clip(jax.random.normal(jax.random.fold_in(key, 24), (DOCS, SEQ, KW), jnp.float32), -4.0, 4.0)
    return values


def draw_partner(key, part):
    offsets = jax.random.randint(jax.random.fold_in(key, 31), (DOCS, 1), 1, N_CTX)
    shards = jnp.arange(N_CTX, dtype=jnp.int32)[None, :]
    return jnp.bitwise_xor(shards, offsets.astype(jnp.int32)).astype(jnp.int32)


def draw_block_mask(key, part):
    levels = jax.random.randint(jax.random.fold_in(key, 32), (DOCS, N_CTX, 1, 1), 1, 9)
    ticks = jax.random.randint(jax.random.fold_in(key, 33), (DOCS, N_CTX, NB, NB), 0, 8)
    return (ticks < levels).astype(jnp.int32)


def block_scale(stream_key, extent, split, low, largest):
    level, own = 1.0, jax.random.fold_in(stream_key, 6)
    for position, shards_of in split:
        draws = jnp.exp(jax.random.uniform(jax.random.fold_in(own, position), (shards_of,), jnp.float32, low / len(split), largest / len(split)))
        level = level * jnp.repeat(draws, extent[position] // shards_of).reshape([-1 if axis == position else 1 for axis in range(len(extent))])
    return level


def normal_values(own_key, extent, deviation, bound, split=(), kind=jnp.bfloat16):
    array = jax.random.normal(own_key, extent, jnp.float32) * deviation
    if len(split) > 0:
        array = block_scale(own_key, extent, split, -0.22, 0.18) * array
    return jnp.clip(array, min=-bound, max=bound).astype(kind)


def setup_inputs(seed: int = 0) -> dict:
    key_of = jax.random.split(jax.random.key(seed), 7)
    return {
        "activations": draw_activations(jax.random.fold_in(key_of[6], 71), 0),
        "queries": draw_queries(jax.random.fold_in(key_of[6], 71), 0),
        "d_out": normal_values(key_of[2], (DOCS, SEQ, KW), 1.0, 6.0, ((0, 2), (1, 16)), jnp.float32),
        "w_kv": draw_w_kv(jax.random.fold_in(key_of[6], 71), 0),
        "partner": draw_partner(jax.random.fold_in(key_of[6], 71), 0),
        "block_mask": draw_block_mask(jax.random.fold_in(key_of[6], 71), 0),
    }


highest = lax.Precision.HIGHEST
masked_score = -1e+30

def visible_keys(mask_blocks, count):
    block = count // mask_blocks.shape[0]
    partner_part = jnp.repeat(jnp.repeat(mask_blocks, block, axis=0), block, axis=1) == 1
    return jnp.concatenate([jnp.ones((count, count), jnp.bool_), partner_part], axis=1)

def attend_shard(query_rows, key_rows, value_rows, visible, cotangent):
    factor = 1.0 / math.sqrt(query_rows.shape[2])
    scores = jnp.einsum('qhd,khd->hqk', query_rows, key_rows, precision=highest) * factor
    scores = jnp.where(visible[None], scores, masked_score)
    maximum = lax.optimization_barrier(jnp.max(scores, axis=2, keepdims=True))
    raised = jnp.exp(scores - maximum)
    totals = lax.optimization_barrier(jnp.sum(raised, axis=2, keepdims=True))
    weights = raised / totals
    attended = jnp.einsum('hqk,khd->qhd', weights, value_rows, precision=highest)
    grad_weights = jnp.einsum('qhd,khd->hqk', cotangent, value_rows, precision=highest)
    row_dot = jnp.transpose(lax.optimization_barrier(jnp.sum(cotangent * attended, axis=2)))[:, :, None]
    grad_scores = weights * (grad_weights - row_dot)
    grad_keys = jnp.einsum('hqk,qhd->khd', grad_scores, query_rows, precision=highest) * factor
    grad_values = jnp.einsum('hqk,qhd->khd', weights, cotangent, precision=highest)
    return (attended, grad_keys, grad_values)

def reference(activations, queries, d_out, w_kv, partner, block_mask):
    width = queries.shape[2]
    heads = width // HEAD

    def one_document(carry, inputs):
        doc_rows, doc_queries, doc_grads, doc_partner, doc_mask = inputs
        pairs = jnp.dot(doc_rows, w_kv, precision=highest)
        shards = pairs.reshape(N_CTX, TOK_DEV, 2 * width)

        def one_shard(shard):
            other = doc_partner[shard].astype(jnp.int32)
            own_pairs = lax.dynamic_index_in_dim(shards, shard, 0, keepdims=False)
            far_pairs = lax.dynamic_index_in_dim(shards, other, 0, keepdims=False)
            joined = jnp.concatenate([own_pairs, far_pairs], axis=0)
            key_rows = joined[:, :width].reshape(2 * TOK_DEV, heads, HEAD)
            value_rows = joined[:, width:].reshape(2 * TOK_DEV, heads, HEAD)
            start = (shard * TOK_DEV).astype(jnp.int32)
            query_rows = lax.dynamic_slice_in_dim(doc_queries, start, TOK_DEV, 0).reshape(TOK_DEV, heads, HEAD)
            cotangent = lax.dynamic_slice_in_dim(doc_grads, start, TOK_DEV, 0).reshape(TOK_DEV, heads, HEAD)
            visible = visible_keys(lax.dynamic_index_in_dim(doc_mask, shard, 0, keepdims=False), TOK_DEV)
            attended, grad_keys, grad_values = attend_shard(query_rows, key_rows, value_rows, visible, cotangent)
            grad_pairs = jnp.concatenate([grad_keys.reshape(2 * TOK_DEV, width), grad_values.reshape(2 * TOK_DEV, width)], axis=1)
            return (attended.reshape(TOK_DEV, width), grad_pairs)
        attended, grad_pairs = lax.map(one_shard, jnp.arange(N_CTX, dtype=jnp.int32))
        own_grads = grad_pairs[:, :TOK_DEV]
        far_grads = grad_pairs[:, TOK_DEV:]
        summed = own_grads + far_grads[doc_partner.astype(jnp.int32)]
        term = jnp.dot(jnp.transpose(doc_rows), summed.reshape(SEQ, 2 * width), precision=highest)
        return (carry + term, attended.reshape(SEQ, width))
    start_sum = jnp.zeros((D, 2 * KW), jnp.float32)
    grad_sum, attended = lax.scan(one_document, start_sum, (activations, queries, d_out, partner, block_mask))
    return (attended, grad_sum * (1.0 / math.sqrt(TOKENS)))
```

```python
import functools
import math

import jax
import jax.numpy as jnp
from jax import lax
from jax.experimental import pallas as pl
from jax.experimental.pallas import tpu as pltpu
from jax.sharding import PartitionSpec as P

HEAD = 64
LANES = 128
MASKED = -1e30
F32 = jnp.float32
BF16 = jnp.bfloat16
VMEM_BYTES = 60 * 1024 * 1024


def split(x):
    high = x.astype(BF16)
    low = (x - high.astype(F32)).astype(BF16)
    return high, low


def dot_nn(a, b):
    return lax.dot_general(a, b, (((1,), (0,)), ((), ())), preferred_element_type=F32)


def dot_nt(a, b):
    return lax.dot_general(a, b, (((1,), (1,)), ((), ())), preferred_element_type=F32)


def halves(x):
    high = x.astype(BF16).astype(F32)
    low = x - high
    return high, low, pltpu.roll(high, HEAD, 1), pltpu.roll(low, HEAD, 1)


def lane_is_low(shape):
    return lax.broadcasted_iota(jnp.int32, shape, 1) < HEAD


def key_packs(x):
    high, low, high_r, low_r = halves(x)
    first = lane_is_low(x.shape)
    pair = high.astype(BF16)
    even = jnp.where(first, high, low_r).astype(BF16)
    odd = jnp.where(first, high_r, low).astype(BF16)
    return jnp.concatenate([even, pair], axis=1), jnp.concatenate([odd, pair], axis=1)


def query_packs(x):
    high, low, high_r, _ = halves(x)
    first = lane_is_low(x.shape)
    zero = jnp.zeros_like(x)
    even = jnp.concatenate(
        [jnp.where(first, high, high_r).astype(BF16), jnp.where(first, low, zero).astype(BF16)], axis=1
    )
    odd = jnp.concatenate(
        [jnp.where(first, high_r, high).astype(BF16), jnp.where(first, zero, low).astype(BF16)], axis=1
    )
    return even, odd


def row_packs(x):
    high, low, high_r, low_r = halves(x)
    first = lane_is_low(x.shape)
    zero = jnp.zeros_like(x)
    even = jnp.concatenate(
        [jnp.where(first, high, low_r).astype(BF16), jnp.where(first, high, zero).astype(BF16)], axis=0
    )
    odd = jnp.concatenate(
        [jnp.where(first, low_r, high).astype(BF16), jnp.where(first, zero, high).astype(BF16)], axis=0
    )
    return even, odd


def project(x_hi, x_lo, w_hi, w_lo, out_ref, columns):
    out_ref[:, columns] = (
        dot_nn(x_hi[...], w_hi[:, columns])
        + dot_nn(x_hi[...], w_lo[:, columns])
        + dot_nn(x_lo[...], w_hi[:, columns])
    )


def transposed(x_ref, me, out_hi, out_lo, blocks):
    depth = x_ref.shape[1]
    size = depth // blocks
    for tile in range(depth // LANES):
        turned = jnp.transpose(x_ref[:, tile * LANES : (tile + 1) * LANES])
        high, low = split(turned)
        for part in range(LANES // size):
            relative = jnp.bitwise_xor(tile * (LANES // size) + part, me)
            place = (relative % 2) * (blocks // 2) + relative // 2
            rows = pl.ds(pl.multiple_of(place * size, size), size)
            out_hi[rows, :] = high[part * size : (part + 1) * size]
            out_lo[rows, :] = low[part * size : (part + 1) * size]


def own_kernel(
    blocks, me_ref, x_ref, w_ref, q_ref, c_ref,
    w_hi, w_lo, xt_hi, xt_lo, value_ref, e_ref, g_ref, stats_ref,
    x_hi, x_lo, pairs,
):
    width = q_ref.shape[1]
    depth = w_ref.shape[0]
    step = 256
    x_hi[...], x_lo[...] = split(x_ref[...])

    @pl.loop(0, depth // step)
    def _(i):
        rows = pl.ds(pl.multiple_of(i * step, step), step)
        w_hi[rows, :], w_lo[rows, :] = split(w_ref[rows, :])

    @pl.loop(0, w_ref.shape[1] // step)
    def _(j):
        project(x_hi, x_lo, w_hi, w_lo, pairs, pl.ds(pl.multiple_of(j * step, step), step))

    value_ref[...] = pairs[:, width:]
    transposed(x_ref, me_ref[0], xt_hi, xt_lo, blocks)

    @pl.loop(0, width // LANES)
    def _(p):
        lanes = pl.ds(pl.multiple_of(p * LANES, LANES), LANES)
        value_lanes = pl.ds(pl.multiple_of(width + p * LANES, LANES), LANES)
        keys = key_packs(pairs[:, lanes])
        values = key_packs(pairs[:, value_lanes])
        queries = query_packs(q_ref[:, lanes] * (1.0 / math.sqrt(HEAD)))
        cotangents = query_packs(c_ref[:, lanes])
        for one in range(2):
            head = 2 * p + one
            scores = dot_nt(keys[one], queries[one])
            maximum = jnp.max(scores, axis=0, keepdims=True)
            raised = jnp.exp(scores - maximum)
            weighed = dot_nt(values[one], cotangents[one])
            e_ref[head] = raised
            g_ref[head] = weighed
            stats_ref[head, 0:1, :] = maximum
            stats_ref[head, 1:2, :] = jnp.sum(raised, axis=0, keepdims=True)
            stats_ref[head, 2:3, :] = jnp.sum(raised * weighed, axis=0, keepdims=True)


def far_kernel(
    blocks, me_ref, mask_ref, x_ref, w_hi, w_lo, q_ref, c_ref, e_ref, g_ref, stats_ref,
    xt_hi, xt_lo, value_ref, grad_hi, grad_lo, p_hi, p_lo,
    x_hi, x_lo, pairs, visible, ds_pack, p_pack,
):
    count, width = q_ref.shape
    step = 256
    n_blocks = mask_ref.shape[0]
    block = count // n_blocks
    x_hi[...], x_lo[...] = split(x_ref[...])

    @pl.loop(0, w_hi.shape[1] // step)
    def _(j):
        project(x_hi, x_lo, w_hi, w_lo, pairs, pl.ds(pl.multiple_of(j * step, step), step))

    value_ref[...] = pairs[:, width:]
    transposed(x_ref, me_ref[0], xt_hi, xt_lo, blocks)

    query_block = lax.broadcasted_iota(jnp.int32, (1, count), 1) // block
    for b in range(n_blocks):
        row = jnp.zeros((1, count), F32)
        for a in range(n_blocks):
            row = jnp.where(query_block == a, mask_ref[a, b].astype(F32), row)
        visible[b : b + 1, :] = row

    @pl.loop(0, width // LANES)
    def _(p):
        lanes = pl.ds(pl.multiple_of(p * LANES, LANES), LANES)
        value_lanes = pl.ds(pl.multiple_of(width + p * LANES, LANES), LANES)
        q_pair = q_ref[:, lanes] * (1.0 / math.sqrt(HEAD))
        c_pair = c_ref[:, lanes]
        keys = key_packs(pairs[:, lanes])
        values = key_packs(pairs[:, value_lanes])
        queries = query_packs(q_pair)
        cotangents = query_packs(c_pair)
        q_rows = row_packs(q_pair)
        c_rows = row_packs(c_pair)
        sums = []
        for one in range(2):
            head = 2 * p + one
            scores = dot_nt(keys[one], queries[one])
            scores = jnp.concatenate(
                [
                    jnp.where(visible[b : b + 1, :] > 0.5, scores[b * block : (b + 1) * block], MASKED)
                    for b in range(n_blocks)
                ],
                axis=0,
            )
            own_maximum = stats_ref[head, 0:1, :]
            maximum = jnp.maximum(jnp.max(scores, axis=0, keepdims=True), own_maximum)
            raised = jnp.exp(scores - maximum)
            weighed = dot_nt(values[one], cotangents[one])
            own_scale = jnp.exp(own_maximum - maximum)
            total = jnp.sum(raised, axis=0, keepdims=True) + own_scale * stats_ref[head, 1:2, :]
            inverse = 1.0 / total
            row_dot = inverse * (
                jnp.sum(raised * weighed, axis=0, keepdims=True) + own_scale * stats_ref[head, 2:3, :]
            )
            for place, (e, g, scale) in enumerate(
                ((e_ref[head], g_ref[head], own_scale * inverse), (raised, weighed, inverse))
            ):
                weights = e * scale
                grads = weights * (g - row_dot)
                rows = slice(place * count, (place + 1) * count)
                high, low = split(weights)
                p_hi[head, rows, :] = high
                p_lo[head, rows, :] = low
                p_pack[rows, :count] = high
                p_pack[rows, count:] = low
                high, low = split(grads)
                ds_pack[rows, :count] = high
                ds_pack[rows, count:] = low
            sums.append((dot_nn(ds_pack[...], q_rows[one]), dot_nn(p_pack[...], c_rows[one])))
        for which, where in ((0, lanes), (1, value_lanes)):
            even, odd = sums[0][which], sums[1][which]
            first = lane_is_low(even.shape)
            total = jnp.where(first, even + pltpu.roll(even, HEAD, 1), odd + pltpu.roll(odd, HEAD, 1))
            grad_hi[:, where], grad_lo[:, where] = split(total)


def term_kernel(
    factor, orders, sizes, me_ref, doc_ref, own_hi, own_lo, far_hi, far_lo, grad_hi, grad_lo, *refs
):
    streams = len(sizes)
    outs = refs[:streams]
    xt_hi, xt_lo = refs[streams], refs[streams + 1]
    count = own_hi.shape[1]
    xt_hi[:, :count], xt_hi[:, count:] = own_hi[...], far_hi[...]
    xt_lo[:, :count], xt_lo[:, count:] = own_lo[...], far_lo[...]
    parity = me_ref[0] % 2
    blocks = outs[0].shape[0]
    columns = outs[0].shape[2]
    size = sum(sizes)
    rows = xt_hi.shape[0]
    row_blocks = rows // size
    docs = blocks // row_blocks
    for d in range(docs):
        where = jnp.bitwise_xor(d, doc_ref[0])
        lanes = pl.ds(pl.multiple_of(where * columns, LANES), columns)
        g_hi, g_lo = grad_hi[:, lanes], grad_lo[:, lanes]
        total = (dot_nn(xt_hi[...], g_hi) + dot_nn(xt_hi[...], g_lo) + dot_nn(xt_lo[...], g_hi)) * factor
        for r in range(row_blocks):
            start = r * size
            for stream in range(streams):
                places = [order_place(order, r, d) for order in orders[stream]]
                place = jnp.where(parity == 0, places[0], places[1])
                outs[stream][place] = total[start : start + sizes[stream]]
                start += sizes[stream]


def order_place(order, row_block, doc_block):
    place = 0
    for axis, bit in order:
        place = place * 2 + ((doc_block >> bit) if axis == "doc" else (row_block >> (bit - 1))) % 2
    return place


def compiler(**more):
    return pltpu.CompilerParams(vmem_limit_bytes=VMEM_BYTES, **more)


VMEM = pl.BlockSpec(memory_space=pltpu.VMEM)
SMEM = pl.BlockSpec(memory_space=pltpu.SMEM)


def shape_of(shape, dtype=F32):
    return jax.ShapeDtypeStruct(shape, dtype)


def own_part(me, x, w, q, c, blocks):
    count, depth = x.shape
    width = q.shape[1]
    heads = width // HEAD
    return pl.pallas_call(
        functools.partial(own_kernel, blocks),
        out_shape=[
            shape_of(w.shape, BF16), shape_of(w.shape, BF16),
            shape_of((depth, count), BF16), shape_of((depth, count), BF16),
            shape_of((count, width)),
            shape_of((heads, count, count)), shape_of((heads, count, count)),
            shape_of((heads, 8, count)),
        ],
        in_specs=[SMEM] + [VMEM] * 4,
        out_specs=[VMEM] * 8,
        scratch_shapes=[
            pltpu.VMEM(x.shape, BF16), pltpu.VMEM(x.shape, BF16), pltpu.VMEM((count, 2 * width), F32),
        ],
        compiler_params=compiler(),
        cost_estimate=pl.CostEstimate(flops=6 * count * depth * 2 * width, bytes_accessed=16 << 20, transcendentals=heads * count * count),
        name="own_part",
    )(me, x, w, q, c)


def far_part(me, mask, x, own, q, c, blocks):
    w_hi, w_lo, _, _, _, e, g, stats = own
    count, depth = x.shape
    width = q.shape[1]
    heads = width // HEAD
    return pl.pallas_call(
        functools.partial(far_kernel, blocks),
        out_shape=[
            shape_of((depth, count), BF16), shape_of((depth, count), BF16),
            shape_of((count, width)),
            shape_of((2 * count, 2 * width), BF16), shape_of((2 * count, 2 * width), BF16),
            shape_of((heads, 2 * count, count), BF16), shape_of((heads, 2 * count, count), BF16),
        ],
        in_specs=[SMEM, SMEM] + [VMEM] * 8,
        out_specs=[VMEM] * 7,
        scratch_shapes=[
            pltpu.VMEM(x.shape, BF16), pltpu.VMEM(x.shape, BF16), pltpu.VMEM((count, 2 * width), F32),
            pltpu.VMEM((8, count), F32),
            pltpu.VMEM((2 * count, 2 * count), BF16), pltpu.VMEM((2 * count, 2 * count), BF16),
        ],
        compiler_params=compiler(),
        name="far_part",
    )(me, mask, x, w_hi, w_lo, q, c, e, g, stats)


def term_part(me, doc, own_t, far_t, grads, half, factor, orders, sizes, docs):
    depth, count = own_t[0].shape
    rows = depth // 2
    columns = grads[0].shape[1] // docs
    blocks = rows // sum(sizes) * docs
    if half:
        orders = [pair[::-1] for pair in orders]
    tall = pl.BlockSpec((rows, count), lambda i: (half, 0))
    return pl.pallas_call(
        functools.partial(term_kernel, factor, orders, sizes),
        grid=(1,),
        out_shape=[shape_of((blocks, size, columns)) for size in sizes],
        in_specs=[SMEM, SMEM] + [tall] * 4 + [VMEM] * 2,
        out_specs=[VMEM] * len(sizes),
        scratch_shapes=[pltpu.VMEM((rows, 2 * count), BF16)] * 2,
        compiler_params=compiler(),
        name="term_part",
    )(me, doc, *own_t, *far_t, *grads)


def attended_kernel(p_hi, p_lo, own_ref, far_ref, out_ref, v_hi, v_lo, turned):
    heads = p_hi.shape[0]
    count = own_ref.shape[0]
    for place, ref in enumerate((own_ref, far_ref)):
        high, low = split(jnp.transpose(ref[...]))
        v_hi[:, place * count : (place + 1) * count] = high
        v_lo[:, place * count : (place + 1) * count] = low

    @pl.loop(0, heads)
    def _(h):
        rows = pl.ds(pl.multiple_of(h * HEAD, HEAD), HEAD)
        turned[rows, :] = (
            dot_nn(v_hi[rows, :], p_hi[h]) + dot_nn(v_lo[rows, :], p_hi[h]) + dot_nn(v_hi[rows, :], p_lo[h])
        )

    out_ref[...] = jnp.transpose(turned[...])


def attended_part(p_hi, p_lo, own_values, far_values):
    count, width = own_values.shape
    return pl.pallas_call(
        attended_kernel,
        out_shape=shape_of((count, width)),
        in_specs=[VMEM] * 4,
        out_specs=VMEM,
        scratch_shapes=[
            pltpu.VMEM((width, 2 * count), BF16), pltpu.VMEM((width, 2 * count), BF16), pltpu.VMEM((width, count), F32),
        ],
        compiler_params=compiler(),
        cost_estimate=pl.CostEstimate(flops=24 * count * count * width, bytes_accessed=6 << 20, transcendentals=0),
        name="attended_part",
    )(p_hi, p_lo, own_values, far_values)


def exchange_along(value, axes):
    n_ctx, n_doc = lax.axis_size("ctx"), lax.axis_size("doc")
    pairs = []
    for i in range(n_ctx):
        for d in range(n_doc):
            axis, bit = axes[i % 2]
            to = (i, d ^ (1 << bit)) if axis == "doc" else (i ^ (1 << bit), d)
            pairs.append((i * n_doc + d, to[0] * n_doc + to[1]))
    return lax.ppermute(value, ("ctx", "doc"), pairs)


def stream_orders(n_ctx, n_doc):
    docs = [("doc", b) for b in reversed(range(n_doc.bit_length() - 1))]
    first = [("ctx", 1)] if n_ctx > 2 else []
    rest = [("ctx", b) for b in range(2, n_ctx.bit_length() - 1)]
    flat = (docs + first + rest, first + docs + rest[::-1])
    tall = (rest + docs + first, rest[::-1] + first + docs)
    return [flat, tall]


def shards(activations, queries, d_out, w_kv, partner, block_mask):
    x, q, c = activations[0], queries[0], d_out[0]
    count, depth = x.shape
    n_ctx, n_doc = lax.axis_size("ctx"), lax.axis_size("doc")
    index = lax.axis_index("ctx").astype(jnp.int32)
    me = index.reshape(1)
    doc = lax.axis_index("doc").astype(jnp.int32).reshape(1)
    offset = jnp.bitwise_xor(partner[0, 0], index)

    def swap(mask, x, w, q, c, me):
        own = own_part(me, x, w, q, c, n_ctx)
        far = lax.ppermute(x, "ctx", [(i, i ^ mask) for i in range(n_ctx)])
        return far, own

    far, own = lax.switch(
        offset - 1, [functools.partial(swap, mask) for mask in range(1, n_ctx)], x, w_kv, q, c, me
    )
    far_hi, far_lo, far_values, grad_hi, grad_lo, p_hi, p_lo = far_part(me, block_mask[0, 0], far, own, q, c, n_ctx)
    own_t, far_t = own[2:4], (far_hi, far_lo)
    factor = 1.0 / math.sqrt(count * n_ctx * n_doc)

    size = depth // n_ctx
    second = size * 3 // 8 // 8 * 8
    sizes = [size - second, second]
    orders = stream_orders(n_ctx, n_doc)
    term = functools.partial(term_part, me, doc, own_t, far_t, (grad_hi, grad_lo))
    send = term(1, factor, orders, sizes, n_doc)
    keep = term(0, factor, orders, sizes, n_doc)
    attended = attended_part(p_hi, p_lo, own[4], far_values)
    core = (("ctx", 0), ("ctx", 0))
    upper, lower = [], []
    for there, here in zip(send, keep):
        half = there.shape[0] // 2
        upper.append(here[half:] + exchange_along(there[half:], core))
    for there, here in zip(send, keep):
        half = there.shape[0] // 2
        lower.append(here[:half] + exchange_along(there[:half], core))
    for level in range(len(orders[0][0])):
        got = [exchange_along(u, (o[0][level], o[1][level])) for u, o in zip(upper, orders)]
        sums = [low + g for low, g in zip(lower, got)]
        half = sums[0].shape[0] // 2
        upper = [s[half:] for s in sums]
        lower = [s[:half] for s in sums] if half else sums
    gradient = jnp.concatenate([s[0] for s in sums], axis=0)
    return attended[None], gradient


def solution(mesh):
    placed = (
        P("doc", "ctx", None),
        P("doc", "ctx", None),
        P("doc", "ctx", None),
        P(),
        P("doc", "ctx"),
        P("doc", "ctx", None, None),
    )
    return jax.shard_map(
        shards,
        mesh=mesh,
        in_specs=placed,
        out_specs=(P("doc", "ctx", None), P("ctx", "doc")),
        check_vma=False,
    )
```

```python
import functools
import math

import jax
import jax.numpy as jnp
from jax import lax
from jax.experimental import pallas as pl
from jax.experimental.pallas import tpu as pltpu
from jax.sharding import PartitionSpec as P

HEAD = 64
LANES = 128
MASKED = -1e30
F32 = jnp.float32
BF16 = jnp.bfloat16


def split(x):
    high = x.astype(BF16)
    low = (x - high.astype(F32)).astype(BF16)
    return high, low


def dot_nn(a, b):
    return lax.dot_general(a, b, (((1,), (0,)), ((), ())), preferred_element_type=F32)


def dot_nt(a, b):
    return lax.dot_general(a, b, (((1,), (1,)), ((), ())), preferred_element_type=F32)


def halves(x):
    high = x.astype(BF16).astype(F32)
    low = x - high
    return high, low, pltpu.roll(high, HEAD, 1), pltpu.roll(low, HEAD, 1)


def lane_is_low(shape):
    return lax.broadcasted_iota(jnp.int32, shape, 1) < HEAD


def key_packs(x):
    high, low, high_r, low_r = halves(x)
    first = lane_is_low(x.shape)
    pair = high.astype(BF16)
    even = jnp.where(first, high, low_r).astype(BF16)
    odd = jnp.where(first, high_r, low).astype(BF16)
    return jnp.concatenate([even, pair], axis=1), jnp.concatenate([odd, pair], axis=1)


def query_packs(x):
    high, low, high_r, _ = halves(x)
    first = lane_is_low(x.shape)
    zero = jnp.zeros_like(x)
    even = jnp.concatenate(
        [jnp.where(first, high, high_r).astype(BF16), jnp.where(first, low, zero).astype(BF16)], axis=1
    )
    odd = jnp.concatenate(
        [jnp.where(first, high_r, high).astype(BF16), jnp.where(first, zero, low).astype(BF16)], axis=1
    )
    return even, odd


def row_packs(x):
    high, low, high_r, low_r = halves(x)
    first = lane_is_low(x.shape)
    zero = jnp.zeros_like(x)
    even = jnp.concatenate(
        [jnp.where(first, high, low_r).astype(BF16), jnp.where(first, high, zero).astype(BF16)], axis=0
    )
    odd = jnp.concatenate(
        [jnp.where(first, low_r, high).astype(BF16), jnp.where(first, zero, high).astype(BF16)], axis=0
    )
    return even, odd


def project(x_hi, x_lo, w_hi, w_lo, out_ref, columns):
    out_ref[:, columns] = (
        dot_nn(x_hi[...], w_hi[:, columns])
        + dot_nn(x_hi[...], w_lo[:, columns])
        + dot_nn(x_lo[...], w_hi[:, columns])
    )


def transposed(x_ref, me, out_hi, out_lo, blocks):
    depth = x_ref.shape[1]
    size = depth // blocks
    for tile in range(depth // LANES):
        turned = jnp.transpose(x_ref[:, tile * LANES : (tile + 1) * LANES])
        high, low = split(turned)
        for part in range(LANES // size):
            relative = jnp.bitwise_xor(tile * (LANES // size) + part, me)
            place = (relative % 2) * (blocks // 2) + relative // 2
            rows = pl.ds(pl.multiple_of(place * size, size), size)
            out_hi[rows, :] = high[part * size : (part + 1) * size]
            out_lo[rows, :] = low[part * size : (part + 1) * size]


def own_kernel(
    blocks, me_ref, x_ref, w_ref, q_ref, c_ref,
    w_hi, w_lo, xt_hi, xt_lo, value_ref, e_ref, g_ref, stats_ref,
    x_hi, x_lo, pairs,
):
    width = q_ref.shape[1]
    depth = w_ref.shape[0]
    step = 256
    x_hi[...], x_lo[...] = split(x_ref[...])

    @pl.loop(0, depth // step)
    def _(i):
        rows = pl.ds(pl.multiple_of(i * step, step), step)
        w_hi[rows, :], w_lo[rows, :] = split(w_ref[rows, :])

    @pl.loop(0, w_ref.shape[1] // step)
    def _(j):
        project(x_hi, x_lo, w_hi, w_lo, pairs, pl.ds(pl.multiple_of(j * step, step), step))

    value_ref[...] = pairs[:, width:]
    transposed(x_ref, me_ref[0], xt_hi, xt_lo, blocks)

    @pl.loop(0, width // LANES)
    def _(p):
        lanes = pl.ds(pl.multiple_of(p * LANES, LANES), LANES)
        value_lanes = pl.ds(pl.multiple_of(width + p * LANES, LANES), LANES)
        keys = key_packs(pairs[:, lanes])
        values = key_packs(pairs[:, value_lanes])
        queries = query_packs(q_ref[:, lanes] * (1.0 / math.sqrt(HEAD)))
        cotangents = query_packs(c_ref[:, lanes])
        for one in range(2):
            head = 2 * p + one
            scores = dot_nt(keys[one], queries[one])
            maximum = jnp.max(scores, axis=0, keepdims=True)
            raised = jnp.exp(scores - maximum)
            weighed = dot_nt(values[one], cotangents[one])
            e_ref[head] = raised
            g_ref[head] = weighed
            stats_ref[head, 0:1, :] = maximum
            stats_ref[head, 1:2, :] = jnp.sum(raised, axis=0, keepdims=True)
            stats_ref[head, 2:3, :] = jnp.sum(raised * weighed, axis=0, keepdims=True)


def far_kernel(
    blocks, me_ref, mask_ref, x_ref, w_hi, w_lo, q_ref, c_ref, e_ref, g_ref, stats_ref,
    xt_hi, xt_lo, value_ref, grad_hi, grad_lo, p_hi, p_lo,
    x_hi, x_lo, pairs, visible, ds_pack, p_pack,
):
    count, width = q_ref.shape
    step = 256
    n_blocks = mask_ref.shape[0]
    block = count // n_blocks
    x_hi[...], x_lo[...] = split(x_ref[...])

    @pl.loop(0, w_hi.shape[1] // step)
    def _(j):
        project(x_hi, x_lo, w_hi, w_lo, pairs, pl.ds(pl.multiple_of(j * step, step), step))

    value_ref[...] = pairs[:, width:]
    transposed(x_ref, me_ref[0], xt_hi, xt_lo, blocks)

    query_block = lax.broadcasted_iota(jnp.int32, (1, count), 1) // block
    for b in range(n_blocks):
        row = jnp.zeros((1, count), F32)
        for a in range(n_blocks):
            row = jnp.where(query_block == a, mask_ref[a, b].astype(F32), row)
        visible[b : b + 1, :] = row

    @pl.loop(0, width // LANES)
    def _(p):
        lanes = pl.ds(pl.multiple_of(p * LANES, LANES), LANES)
        value_lanes = pl.ds(pl.multiple_of(width + p * LANES, LANES), LANES)
        q_pair = q_ref[:, lanes] * (1.0 / math.sqrt(HEAD))
        c_pair = c_ref[:, lanes]
        keys = key_packs(pairs[:, lanes])
        values = key_packs(pairs[:, value_lanes])
        queries = query_packs(q_pair)
        cotangents = query_packs(c_pair)
        q_rows = row_packs(q_pair)
        c_rows = row_packs(c_pair)
        sums = []
        for one in range(2):
            head = 2 * p + one
            scores = dot_nt(keys[one], queries[one])
            scores = jnp.concatenate(
                [
                    jnp.where(visible[b : b + 1, :] > 0.5, scores[b * block : (b + 1) * block], MASKED)
                    for b in range(n_blocks)
                ],
                axis=0,
            )
            own_maximum = stats_ref[head, 0:1, :]
            maximum = jnp.maximum(jnp.max(scores, axis=0, keepdims=True), own_maximum)
            raised = jnp.exp(scores - maximum)
            weighed = dot_nt(values[one], cotangents[one])
            own_scale = jnp.exp(own_maximum - maximum)
            total = jnp.sum(raised, axis=0, keepdims=True) + own_scale * stats_ref[head, 1:2, :]
            inverse = 1.0 / total
            row_dot = inverse * (
                jnp.sum(raised * weighed, axis=0, keepdims=True) + own_scale * stats_ref[head, 2:3, :]
            )
            for place, (e, g, scale) in enumerate(
                ((e_ref[head], g_ref[head], own_scale * inverse), (raised, weighed, inverse))
            ):
                weights = e * scale
                grads = weights * (g - row_dot)
                rows = slice(place * count, (place + 1) * count)
                high, low = split(weights)
                p_hi[head, rows, :] = high
                p_lo[head, rows, :] = low
                p_pack[rows, :count] = high
                p_pack[rows, count:] = low
                high, low = split(grads)
                ds_pack[rows, :count] = high
                ds_pack[rows, count:] = low
            sums.append((dot_nn(ds_pack[...], q_rows[one]), dot_nn(p_pack[...], c_rows[one])))
        for which, where in ((0, lanes), (1, value_lanes)):
            even, odd = sums[0][which], sums[1][which]
            first = lane_is_low(even.shape)
            total = jnp.where(first, even + pltpu.roll(even, HEAD, 1), odd + pltpu.roll(odd, HEAD, 1))
            grad_hi[:, where], grad_lo[:, where] = split(total)


def term_kernel(
    factor, orders, sizes, me_ref, doc_ref, own_hi, own_lo, far_hi, far_lo, grad_hi, grad_lo, *refs
):
    streams = len(sizes)
    outs = refs[:streams]
    xt_hi, xt_lo = refs[streams], refs[streams + 1]
    count = own_hi.shape[1]
    xt_hi[:, :count], xt_hi[:, count:] = own_hi[...], far_hi[...]
    xt_lo[:, :count], xt_lo[:, count:] = own_lo[...], far_lo[...]
    parity = me_ref[0] % 2
    blocks = outs[0].shape[0]
    columns = outs[0].shape[2]
    size = sum(sizes)
    rows = xt_hi.shape[0]
    row_blocks = rows // size
    docs = blocks // row_blocks
    for d in range(docs):
        where = jnp.bitwise_xor(d, doc_ref[0])
        lanes = pl.ds(pl.multiple_of(where * columns, LANES), columns)
        g_hi, g_lo = grad_hi[:, lanes], grad_lo[:, lanes]
        total = (dot_nn(xt_hi[...], g_hi) + dot_nn(xt_hi[...], g_lo) + dot_nn(xt_lo[...], g_hi)) * factor
        for r in range(row_blocks):
            start = r * size
            for stream in range(streams):
                places = [order_place(order, r, d) for order in orders[stream]]
                place = jnp.where(parity == 0, places[0], places[1])
                outs[stream][place] = total[start : start + sizes[stream]]
                start += sizes[stream]


def order_place(order, row_block, doc_block):
    place = 0
    for axis, bit in order:
        place = place * 2 + ((doc_block >> bit) if axis == "doc" else (row_block >> (bit - 1))) % 2
    return place


def compiler(mebibytes):
    return pltpu.CompilerParams(vmem_limit_bytes=mebibytes << 20)


VMEM = pl.BlockSpec(memory_space=pltpu.VMEM)
SMEM = pl.BlockSpec(memory_space=pltpu.SMEM)


def shape_of(shape, dtype=F32):
    return jax.ShapeDtypeStruct(shape, dtype)


def own_part(me, x, w, q, c, blocks):
    count, depth = x.shape
    width = q.shape[1]
    heads = width // HEAD
    return pl.pallas_call(
        functools.partial(own_kernel, blocks),
        out_shape=[
            shape_of(w.shape, BF16), shape_of(w.shape, BF16),
            shape_of((depth, count), BF16), shape_of((depth, count), BF16),
            shape_of((count, width)),
            shape_of((heads, count, count)), shape_of((heads, count, count)),
            shape_of((heads, 8, count)),
        ],
        in_specs=[SMEM] + [VMEM] * 4,
        out_specs=[VMEM] * 8,
        scratch_shapes=[
            pltpu.VMEM(x.shape, BF16), pltpu.VMEM(x.shape, BF16), pltpu.VMEM((count, 2 * width), F32),
        ],
        compiler_params=compiler(21),
        cost_estimate=pl.CostEstimate(flops=6 * count * depth * 2 * width, bytes_accessed=16 << 20, transcendentals=heads * count * count),
        name="own_part",
    )(me, x, w, q, c)


def far_part(me, mask, x, own, q, c, blocks):
    w_hi, w_lo, _, _, _, e, g, stats = own
    count, depth = x.shape
    width = q.shape[1]
    heads = width // HEAD
    return pl.pallas_call(
        functools.partial(far_kernel, blocks),
        out_shape=[
            shape_of((depth, count), BF16), shape_of((depth, count), BF16),
            shape_of((count, width)),
            shape_of((2 * count, 2 * width), BF16), shape_of((2 * count, 2 * width), BF16),
            shape_of((heads, 2 * count, count), BF16), shape_of((heads, 2 * count, count), BF16),
        ],
        in_specs=[SMEM, SMEM] + [VMEM] * 8,
        out_specs=[VMEM] * 7,
        scratch_shapes=[
            pltpu.VMEM(x.shape, BF16), pltpu.VMEM(x.shape, BF16), pltpu.VMEM((count, 2 * width), F32),
            pltpu.VMEM((8, count), F32),
            pltpu.VMEM((2 * count, 2 * count), BF16), pltpu.VMEM((2 * count, 2 * count), BF16),
        ],
        compiler_params=compiler(26),
        name="far_part",
    )(me, mask, x, w_hi, w_lo, q, c, e, g, stats)


def term_part(me, doc, own_t, far_t, grads, half, factor, orders, sizes, docs):
    depth, count = own_t[0].shape
    rows = depth // 2
    columns = grads[0].shape[1] // docs
    blocks = rows // sum(sizes) * docs
    if half:
        orders = [pair[::-1] for pair in orders]
    tall = pl.BlockSpec((rows, count), lambda i: (half, 0))
    return pl.pallas_call(
        functools.partial(term_kernel, factor, orders, sizes),
        grid=(1,),
        out_shape=[shape_of((blocks, size, columns)) for size in sizes],
        in_specs=[SMEM, SMEM] + [tall] * 4 + [VMEM] * 2,
        out_specs=[VMEM] * len(sizes),
        scratch_shapes=[pltpu.VMEM((rows, 2 * count), BF16)] * 2,
        compiler_params=compiler(12),
        name="term_part",
    )(me, doc, *own_t, *far_t, *grads)


def attended_kernel(p_hi, p_lo, own_ref, far_ref, out_ref, v_hi, v_lo, turned):
    heads = p_hi.shape[0]
    count = own_ref.shape[0]
    for place, ref in enumerate((own_ref, far_ref)):
        high, low = split(jnp.transpose(ref[...]))
        v_hi[:, place * count : (place + 1) * count] = high
        v_lo[:, place * count : (place + 1) * count] = low

    @pl.loop(0, heads)
    def _(h):
        rows = pl.ds(pl.multiple_of(h * HEAD, HEAD), HEAD)
        turned[rows, :] = (
            dot_nn(v_hi[rows, :], p_hi[h]) + dot_nn(v_lo[rows, :], p_hi[h]) + dot_nn(v_hi[rows, :], p_lo[h])
        )

    out_ref[...] = jnp.transpose(turned[...])


def attended_part(p_hi, p_lo, own_values, far_values):
    count, width = own_values.shape
    return pl.pallas_call(
        attended_kernel,
        out_shape=shape_of((count, width)),
        in_specs=[VMEM] * 4,
        out_specs=VMEM,
        scratch_shapes=[
            pltpu.VMEM((width, 2 * count), BF16), pltpu.VMEM((width, 2 * count), BF16), pltpu.VMEM((width, count), F32),
        ],
        compiler_params=compiler(12),
        cost_estimate=pl.CostEstimate(flops=24 * count * count * width, bytes_accessed=6 << 20, transcendentals=0),
        name="attended_part",
    )(p_hi, p_lo, own_values, far_values)


def exchange_along(value, axes):
    n_ctx, n_doc = lax.axis_size("ctx"), lax.axis_size("doc")
    pairs = []
    for i in range(n_ctx):
        for d in range(n_doc):
            axis, bit = axes[i % 2]
            to = (i, d ^ (1 << bit)) if axis == "doc" else (i ^ (1 << bit), d)
            pairs.append((i * n_doc + d, to[0] * n_doc + to[1]))
    return lax.ppermute(value, ("ctx", "doc"), pairs)


def stream_orders(n_ctx, n_doc):
    docs = [("doc", b) for b in reversed(range(n_doc.bit_length() - 1))]
    first = [("ctx", 1)] if n_ctx > 2 else []
    rest = [("ctx", b) for b in range(2, n_ctx.bit_length() - 1)]
    flat = (docs + first + rest, first + docs + rest[::-1])
    tall = (rest + docs + first, rest[::-1] + first + docs)
    return [flat, tall]


def shards(activations, queries, d_out, w_kv, partner, block_mask):
    x, q, c = activations[0], queries[0], d_out[0]
    count, depth = x.shape
    n_ctx, n_doc = lax.axis_size("ctx"), lax.axis_size("doc")
    index = lax.axis_index("ctx").astype(jnp.int32)
    me = index.reshape(1)
    doc = lax.axis_index("doc").astype(jnp.int32).reshape(1)
    offset = jnp.bitwise_xor(partner[0, 0], index)

    def swap(mask, x, w, q, c, me):
        own = own_part(me, x, w, q, c, n_ctx)
        far = lax.ppermute(x, "ctx", [(i, i ^ mask) for i in range(n_ctx)])
        return far, own

    far, own = lax.switch(
        offset - 1, [functools.partial(swap, mask) for mask in range(1, n_ctx)], x, w_kv, q, c, me
    )
    far_hi, far_lo, far_values, grad_hi, grad_lo, p_hi, p_lo = far_part(me, block_mask[0, 0], far, own, q, c, n_ctx)
    own_t, far_t = own[2:4], (far_hi, far_lo)
    factor = 1.0 / math.sqrt(count * n_ctx * n_doc)

    size = depth // n_ctx
    second = size * 3 // 8 // 8 * 8
    sizes = [size - second, second]
    orders = stream_orders(n_ctx, n_doc)
    term = functools.partial(term_part, me, doc, own_t, far_t, (grad_hi, grad_lo))
    send = term(1, factor, orders, sizes, n_doc)
    keep = term(0, factor, orders, sizes, n_doc)
    attended = attended_part(p_hi, p_lo, own[4], far_values)
    core = (("ctx", 0), ("ctx", 0))
    upper, lower = [], []
    for there, here in zip(send, keep):
        half = there.shape[0] // 2
        upper.append(here[half:] + exchange_along(there[half:], core))
    for there, here in zip(send, keep):
        half = there.shape[0] // 2
        lower.append(here[:half] + exchange_along(there[:half], core))
    for level in range(len(orders[0][0])):
        got = [exchange_along(u, (o[0][level], o[1][level])) for u, o in zip(upper, orders)]
        sums = [low + g for low, g in zip(lower, got)]
        half = sums[0].shape[0] // 2
        upper = [s[half:] for s in sums]
        lower = [s[:half] for s in sums] if half else sums
    gradient = jnp.concatenate([s[0] for s in sums], axis=0)
    return attended[None], gradient


def solution(mesh):
    placed = (
        P("doc", "ctx", None),
        P("doc", "ctx", None),
        P("doc", "ctx", None),
        P(),
        P("doc", "ctx"),
        P("doc", "ctx", None, None),
    )
    return jax.shard_map(
        shards,
        mesh=mesh,
        in_specs=placed,
        out_specs=(P("doc", "ctx", None), P("ctx", "doc")),
        check_vma=False,
    )
```
